32 devices in a mesh: row: 4 (over x, core), col: 8 (over z, y).
Axes of the slice: x: 2, y: 2, z: 4, core: 2. Of those that a mesh axis runs over, the one named last changes fastest.
Arguments:
- schur: float32 [4096, 4096], P('row', 'col'), may hold values from -6 to 6
- left_rot: float32 [8, 512, 512], P('row', 'col'), may hold values from -1 to 1, as said below
- right_rot: float32 [8, 512, 512], P('col', 'row'), may hold values from -1 to 1, as said below
- left_off: float32 [8, 512, 512], P('row', 'col'), may hold values from -1 to 1, as said below
- right_off: float32 [8, 512, 512], P('col', 'row'), may hold values from -1 to 1, as said below
Outputs:
- updated: float32 [4096, 4096], P('row', 'col')
The draws below stay inside these ranges and needn't reach their ends.
Inputs may be any that keep to these rules, and one draw needn't show every extreme that they name: `left_rot`: each 512 x 512 block is orthogonal. `right_rot`: each 512 x 512 block is orthogonal. `left_off`: each 512 x 512 block is orthogonal. `right_off`: each 512 x 512 block is orthogonal.
All inputs are finite; a program needn't handle non-finite values.
Results may differ from the reference program's by a relative error of at most 0.00007.
Values sent between devices are 32-bit elements; how exact they have to be, the bound alone decides.
A program may use at most 64 MiB of HBM per device.

```python
import jax
import jax.numpy as jnp
from jax import lax

WIN = 512
NROWS = 4096
NCOLS = 4096
LEFT_WINS = 8
RIGHT_WINS = 8


def orthogonal_blocks(key, number):
    base = jax.random.normal(key, (number, WIN, WIN), jnp.float32)
    factor_q, factor_r = jnp.linalg.qr(base)
    signs = jnp.sign(jnp.diagonal(factor_r, axis1=1, axis2=2)) + 0.0
    signs = jnp.where(signs == 0.0, 1.0, signs)
    return factor_q * signs[:, None, :]


def draw_left_rot(key, part):
    return orthogonal_blocks(jax.random.fold_in(key, 11), LEFT_WINS)


def draw_right_rot(key, part):
    return orthogonal_blocks(jax.random.fold_in(key, 23), RIGHT_WINS)


def draw_left_off(key, part):
    return orthogonal_blocks(jax.random.fold_in(key, 37), LEFT_WINS)


def draw_right_off(key, part):
    return orthogonal_blocks(jax.random.fold_in(key, 41), RIGHT_WINS)


def shard_levels(own_key, extent, cuts, low, top_value):
    level = 1.0
    for axis_at, blocks in cuts:
        draws = jax.random.uniform(jax.random.fold_in(jax.random.fold_in(own_key, 6), axis_at), (blocks,), jnp.float32, low / len(cuts), top_value / len(cuts))
        level = level * jnp.repeat(jnp.exp(draws), extent[axis_at] // blocks).reshape((-1,) + (1,) * (len(extent) - 1 - axis_at))
    return level


def noise(key, shape, deviation, limit, pieces=(), held_as=jnp.bfloat16):
    entries = deviation * jax.random.normal(key, shape, jnp.float32)
    if pieces:
        entries = entries * shard_levels(key, shape, pieces, -0.22, 0.18)
    return jnp.clip(entries, -limit, limit).astype(held_as)


def setup_inputs(seed: int = 0) -> dict:
    key_of = jax.random.split(jax.random.key(seed), 6)
    schur = noise(key_of[0], (NROWS, NCOLS), 1.0, 6.0, ((0, 4), (1, 8)), jnp.float32)
    left_rot = draw_left_rot(jax.random.fold_in(key_of[5], 71), 0)
    right_rot = draw_right_rot(jax.random.fold_in(key_of[5], 71), 0)
    left_off = draw_left_off(jax.random.fold_in(key_of[5], 71), 0)
    right_off = draw_right_off(jax.random.fold_in(key_of[5], 71), 0)
    return {"schur": schur, "left_rot": left_rot, "right_rot": right_rot, "left_off": left_off, "right_off": right_off}


def left_apply(matrix, rotations):
    number = rotations.shape[0]
    window = rotations.shape[1]
    shaped = matrix.reshape(number, window, matrix.shape[1])
    result = jnp.einsum('kab,kac->kbc', rotations, shaped, precision=lax.Precision.HIGHEST)
    return result.reshape(matrix.shape)

def right_apply(matrix, rotations):
    number = rotations.shape[0]
    window = rotations.shape[1]
    shaped = matrix.reshape(matrix.shape[0], number, window)
    result = jnp.einsum('rka,kab->rkb', shaped, rotations, precision=lax.Precision.HIGHEST)
    return result.reshape(matrix.shape)

def reference(schur, left_rot, right_rot, left_off, right_off):
    half_window = WIN // 2
    matrix = left_apply(schur, left_rot)
    matrix = right_apply(matrix, right_rot)
    matrix = jnp.roll(matrix, half_window, axis=0)
    matrix = left_apply(matrix, left_off)
    matrix = jnp.roll(matrix, -half_window, axis=0)
    matrix = jnp.roll(matrix, half_window, axis=1)
    matrix = right_apply(matrix, right_off)
    matrix = jnp.roll(matrix, -half_window, axis=1)
    return matrix
```

```python
import functools

import jax
import jax.numpy as jnp
from jax import lax
from jax.experimental import pallas as pl
from jax.experimental.pallas import tpu as pltpu
from jax.sharding import PartitionSpec as P

MESH = pl.DeviceIdType.MESH
F32 = jnp.float32
BF16 = jnp.bfloat16


def run(pred, fn):
    if pred is None:
        fn()
    else:
        pl.when(pred)(fn)


def both(a, b):
    if a is None:
        return b
    if b is None:
        return a
    return jnp.logical_and(a, b)


def split(v):
    high = v.astype(BF16)
    return high, (v - high.astype(F32)).astype(BF16)


def dot3(a, b, dims):
    def one(p, q):
        return lax.dot_general(p, q, (dims, ((), ())), preferred_element_type=F32)

    return one(a[0], b[0]) + (one(a[0], b[1]) + one(a[1], b[0]))


RIGHT = ((1,), (0,))
LEFT = ((0,), (0,))


def kernel(
    R, C, chunk,
    x, rr_in, ro_in, lr_in, lo_in, out,
    rr, ro, nx, lr, lo, nl, m, m2, m3, hp, hn, ha, hb,
    rr_h, rr_l, ro_h, ro_l, nx_h, nx_l,
    rr_s, rr_r, ro_s, ro_r, nx_s, nx_r, lr_s, lr_r, lo_s, lo_r, nl_s, nl_r,
    hp_s, hp_r, hn_s, hn_r, hr_s, hr_r,
):
    r = lax.axis_index("row")
    c = lax.axis_index("col")
    L = C // 2
    line = lax.div(c, 2)
    y = lax.rem(c, 2)
    mate = 2 * line + 1 - y
    c_next, c_prev = lax.rem(c + 1, C), lax.rem(c + C - 1, C)
    r_next, r_prev = lax.rem(r + 1, R), lax.rem(r + R - 1, R)
    can_up, can_down = line < L - 1, line > 0
    c_up, c_down = lax.rem(c + 2, C), lax.rem(c + C - 2, C)
    rows, cols = x.shape
    win = lr_in.shape[2]
    half = win // 2
    nr = rr_in.shape[0]
    nleft = lr_in.shape[0]
    pending = []

    def put(src, dst, ssem, rsem, dev, pred=None):
        def copy():
            return pltpu.make_async_remote_copy(
                src_ref=src(), dst_ref=dst(), send_sem=ssem(), recv_sem=rsem(),
                device_id=dev, device_id_type=MESH,
            )

        run(pred, lambda: copy().start())
        pending.append((pred, lambda: copy().wait_send()))

    def got(dst, rsem, pred=None):
        def wait():
            pltpu.make_async_remote_copy(
                src_ref=dst(), dst_ref=dst(), send_sem=rsem(), recv_sem=rsem(),
                device_id={"col": c_next}, device_id_type=MESH,
            ).wait_recv()

        run(pred, wait)

    barrier = pltpu.get_barrier_semaphore()

    def greet(dev, pred=None):
        run(pred, lambda: pl.semaphore_signal(barrier, inc=1, device_id=dev, device_id_type=MESH))

    for d in range(1, R):
        greet({"row": lax.rem(r + d, R)})
    greet({"col": c_next})
    greet({"col": c_prev})
    greet({"col": c_up}, can_up)
    greet({"col": c_down}, can_down)
    pl.semaphore_wait(barrier, R + 1 + can_up.astype(jnp.int32) + can_down.astype(jnp.int32))

    for d in range(1, R):
        put(lambda: rr_in, lambda: rr.at[r], lambda d=d: rr_s.at[d], lambda: rr_r.at[r],
            {"row": lax.rem(r + d, R)})

    def lr_put(src, j, k, dev, pred):
        put(src, lambda: lr.at[j], lambda: lr_s.at[k, j], lambda: lr_r.at[j], {"col": dev}, pred)

    def lo_put(src, j, k, dev, pred):
        put(src, lambda: lo.at[j], lambda: lo_s.at[k, j], lambda: lo_r.at[j], {"col": dev}, pred)

    def nl_put(src, j, pred):
        put(src, lambda: nl.at[j], lambda: nl_s.at[j], lambda: nl_r.at[j], {"row": r_prev}, pred)

    lr_put(lambda: lr_in, c, 2, mate, None)
    lr_put(lambda: lr_in, c, 0, c_up, can_up)
    lr_put(lambda: lr_in, c, 1, c_down, can_down)
    put(lambda: ro_in.at[0, :, pl.ds(0, half)], lambda: nx.at[r], lambda: nx_s.at[0],
        lambda: nx_r.at[r], {"col": c_prev})
    for d in range(1, R):
        put(lambda: ro_in, lambda: ro.at[r], lambda d=d: ro_s.at[d], lambda: ro_r.at[r],
            {"row": lax.rem(r + d, R)})
    lo_put(lambda: lo_in, c, 2, mate, None)
    lo_put(lambda: lo_in, c, 0, c_up, can_up)
    lo_put(lambda: lo_in, c, 1, c_down, can_down)
    nl_put(lambda: lo_in.at[0, :, pl.ds(0, half)], c, None)
    rr[r] = rr_in[...]
    ro[r] = ro_in[...]
    lr[c] = lr_in[...]
    lo[c] = lo_in[...]

    def lr_pass(j, k, dev, pred):
        lr_put(lambda: lr.at[j], j, k, dev, pred)

    def lr_step(s, par):
        below, above = line - 1 - s, line + 1 + s
        jb = lax.rem(2 * below + par + 2 * C, C)
        ja = lax.rem(2 * above + par, C)
        has_b, has_a = below >= 0, above <= L - 1
        got(lambda: lr.at[jb], lambda: lr_r.at[jb], has_b)
        lr_pass(jb, 0, c_up, both(has_b, can_up))
        got(lambda: lr.at[ja], lambda: lr_r.at[ja], has_a)
        lr_pass(ja, 1, c_down, both(has_a, can_down))

    def lo_step(s):
        below, above = line - 1 - s, line + 1 + s
        jb = lax.rem(2 * below + y + 2 * C, C)
        ja = lax.rem(2 * above + y, C)
        has_b, has_a = below >= 0, above <= L - 1
        for j, has, k, dev, can in (
            (jb, has_b, 0, c_up, can_up), (ja, has_a, 1, c_down, can_down),
        ):
            got(lambda: lo.at[j], lambda: lo_r.at[j], has)
            lo_put(lambda j=j: lo.at[j], j, 2, mate, has)
            lo_put(lambda j=j: lo.at[j], j, k, dev, both(has, can))
            nl_put(lambda j=j: lo.at[j, 0, :, pl.ds(0, half)], j, has)

    got(lambda: lr.at[mate], lambda: lr_r.at[mate])
    lr_pass(mate, 0, c_up, can_up)
    lr_pass(mate, 1, c_down, can_down)
    lr_step(0, y)

    for d in range(1, R):
        q = lax.rem(r + d, R)
        got(lambda: rr.at[q], lambda: rr_r.at[q])
    for w in range(nr):
        h, l = split(rr[:, w].reshape(win, win))
        rr_h[w] = h
        rr_l[w] = l
    n_chunks = rows // chunk

    def span(i):
        return pl.ds(pl.multiple_of(i * chunk, chunk), chunk)

    def halo_copies(i):
        right = pltpu.make_async_remote_copy(
            src_ref=m.at[span(i), pl.ds(cols - half, half)], dst_ref=hp.at[span(i), :],
            send_sem=hp_s.at[i], recv_sem=hp_r.at[i],
            device_id={"col": c_next}, device_id_type=MESH)
        left = pltpu.make_async_remote_copy(
            src_ref=m.at[span(i), pl.ds(0, half)], dst_ref=hn.at[span(i), :],
            send_sem=hn_s.at[i], recv_sem=hn_r.at[i],
            device_id={"col": c_prev}, device_id_type=MESH)
        return right, left

    def right_chunk(i, carry):
        for w in range(nr):
            a = split(x[span(i), pl.ds(w * win, win)])
            m[span(i), pl.ds(w * win, win)] = dot3(a, (rr_h[w], rr_l[w]), RIGHT)
        for copy in halo_copies(i):
            copy.start()
        return carry

    lax.fori_loop(0, n_chunks, right_chunk, 0)

    got(lambda: nx.at[r], lambda: nx_r.at[r])
    for d in range(1, R):
        put(lambda: nx.at[r], lambda: nx.at[r], lambda d=d: nx_s.at[d], lambda: nx_r.at[r],
            {"row": lax.rem(r + d, R)})

    lr_step(0, 1 - y)
    lo_step(0)
    for s in range(1, L - 1):
        lr_step(s, y)
        lr_step(s, 1 - y)
        lo_step(s)

    for d in range(1, R):
        q = lax.rem(r + d, R)
        got(lambda: ro.at[q], lambda: ro_r.at[q])
        got(lambda: nx.at[q], lambda: nx_r.at[q])
    for w in range(nr):
        h, l = split(ro[:, w].reshape(win, win))
        ro_h[w] = h
        ro_l[w] = l
    h, l = split(nx[...].reshape(win, half))
    nx_h[...] = h
    nx_l[...] = l

    def shifted_chunk(i, carry):
        right, left = halo_copies(i)
        right.wait_recv()
        first = split(m[span(i), pl.ds(0, half)])
        ahead = split(hp[span(i), :])
        top = (ro_h[0, :half, half:], ro_l[0, :half, half:])
        low = (ro_h[0, half:, half:], ro_l[0, half:, half:])
        m2[span(i), pl.ds(0, half)] = dot3(ahead, top, RIGHT) + dot3(first, low, RIGHT)
        for w in range(1, nr):
            a = split(m[span(i), pl.ds(w * win - half, win)])
            m2[span(i), pl.ds(w * win - half, win)] = dot3(a, (ro_h[w], ro_l[w]), RIGHT)
        left.wait_recv()
        last = split(m[span(i), pl.ds(cols - half, half)])
        after = split(hn[span(i), :])
        top = (nx_h[:half, :], nx_l[:half, :])
        low = (nx_h[half:, :], nx_l[half:, :])
        m2[span(i), pl.ds(cols - half, half)] = dot3(last, top, RIGHT) + dot3(after, low, RIGHT)
        return carry

    lax.fori_loop(0, n_chunks, shifted_chunk, 0)

    def left_window(k, carry):
        at = pl.ds(pl.multiple_of(k * win, win), win)
        q = split(lr[:, k].reshape(win, win))
        for w in range(cols // win):
            across = pl.ds(w * win, win)
            m3[at, across] = dot3(q, split(m2[at, across]), LEFT)
        return carry

    lax.fori_loop(0, nleft, left_window, 0)
    put(lambda: m3.at[pl.ds(rows - half, half), :], lambda: ha, lambda: hr_s.at[0],
        lambda: hr_r.at[0], {"row": r_next})
    put(lambda: m3.at[pl.ds(0, half), :], lambda: hb, lambda: hr_s.at[1],
        lambda: hr_r.at[1], {"row": r_prev})

    for g in range(L):
        j = 2 * g + 1 - y
        got(lambda: lo.at[j], lambda: lo_r.at[j])
        nl_put(lambda j=j: lo.at[j, 0, :, pl.ds(0, half)], j, None)

    def shifted_left(k, carry):
        at = pl.ds(pl.multiple_of(k * win - half, half), win)
        q = split(lo[:, k].reshape(win, win))
        for w in range(cols // win):
            across = pl.ds(w * win, win)
            out[at, across] = dot3(q, split(m3[at, across]), LEFT)
        return carry

    lax.fori_loop(1, nleft, shifted_left, 0)
    got(lambda: ha, lambda: hr_r.at[0])
    q = split(lo[:, 0].reshape(win, win)[:, half:])
    for w in range(cols // win):
        across = pl.ds(w * win, win)
        out[pl.ds(0, half), across] = dot3(
            (q[0][:half], q[1][:half]), split(ha[:, across]), LEFT
        ) + dot3((q[0][half:], q[1][half:]), split(m3[pl.ds(0, half), across]), LEFT)
    for j in range(C):
        got(lambda: nl.at[j], lambda: nl_r.at[j])
    got(lambda: hb, lambda: hr_r.at[1])
    q = split(nl[...].reshape(win, half))
    for w in range(cols // win):
        across = pl.ds(w * win, win)
        out[pl.ds(rows - half, half), across] = dot3(
            (q[0][:half], q[1][:half]), split(m3[pl.ds(rows - half, half), across]), LEFT
        ) + dot3((q[0][half:], q[1][half:]), split(hb[:, across]), LEFT)

    def sent(i, carry):
        for copy in halo_copies(i):
            copy.wait_send()
        return carry

    lax.fori_loop(0, n_chunks, sent, 0)
    for pred, wait in pending:
        run(pred, wait)


def solution(mesh):
    R, C = mesh.shape["row"], mesh.shape["col"]

    def body(schur, left_rot, right_rot, left_off, right_off):
        rows, cols = schur.shape
        win = left_rot.shape[2]
        half = win // 2
        nr, nleft = right_rot.shape[0], left_rot.shape[0]
        chunk = half
        n_chunks = rows // chunk
        dma = pltpu.SemaphoreType.DMA
        vm = pltpu.VMEM
        right = (R,) + right_rot.shape
        left = (C,) + left_rot.shape
        return pl.pallas_call(
            functools.partial(kernel, R, C, chunk),
            out_shape=jax.ShapeDtypeStruct((rows, cols), F32),
            in_specs=[pl.BlockSpec(memory_space=vm)] * 5,
            out_specs=pl.BlockSpec(memory_space=vm),
            scratch_shapes=[
                vm(right, F32), vm(right, F32), vm((R, win // R, half), F32),
                vm(left, F32), vm(left, F32), vm((C, win // C, half), F32),
                vm((rows, cols), F32), vm((rows, cols), F32), vm((rows, cols), F32),
                vm((rows, half), F32), vm((rows, half), F32),
                vm((half, cols), F32), vm((half, cols), F32),
                vm((nr, win, win), BF16), vm((nr, win, win), BF16),
                vm((nr, win, win), BF16), vm((nr, win, win), BF16),
                vm((win, half), BF16), vm((win, half), BF16),
                dma((R,)), dma((R,)), dma((R,)), dma((R,)), dma((R,)), dma((R,)),
                dma((3, C)), dma((C,)), dma((3, C)), dma((C,)), dma((C,)), dma((C,)),
                dma((n_chunks,)), dma((n_chunks,)), dma((n_chunks,)), dma((n_chunks,)),
                dma((2,)), dma((2,)),
            ],
            compiler_params=pltpu.CompilerParams(collective_id=0, has_side_effects=True),
        )(schur, right_rot, right_off, left_rot, left_off)

    return jax.shard_map(
        body,
        mesh=mesh,
        in_specs=(
            P("row", "col"),
            P("row", "col", None),
            P("col", "row", None),
            P("row", "col", None),
            P("col", "row", None),
        ),
        out_specs=P("row", "col"),
        check_vma=False,
    )
```

```python
import functools

import jax
import jax.numpy as jnp
from jax import lax
from jax.experimental import pallas as pl
from jax.experimental.pallas import tpu as pltpu
from jax.sharding import PartitionSpec as P

MESH = pl.DeviceIdType.MESH
F32 = jnp.float32
BF16 = jnp.bfloat16


def run(pred, fn):
    if pred is None:
        fn()
    else:
        pl.when(pred)(fn)


def both(a, b):
    if a is None:
        return b
    if b is None:
        return a
    return jnp.logical_and(a, b)


def split(v):
    high = v.astype(BF16)
    return high, (v - high.astype(F32)).astype(BF16)


def dot3(a, b, dims):
    def one(p, q):
        return lax.dot_general(p, q, (dims, ((), ())), preferred_element_type=F32)

    return one(a[0], b[0]) + (one(a[0], b[1]) + one(a[1], b[0]))


RIGHT = ((1,), (0,))
LEFT = ((0,), (0,))


def kernel(
    R, C, chunk,
    x_in, rr_in, ro_in, lr_in, lo_in, out,
    x, rr, ro, nx, lr, lo, nl, m, m2, m3, hp, hn, ha, hb,
    rr_h, rr_l, ro_h, ro_l, nx_h, nx_l,
    rr_s, rr_r, ro_s, ro_r, nx_s, nx_r, lr_s, lr_r, lo_s, lo_r, nl_s, nl_r,
    hp_s, hp_r, hn_s, hn_r, hr_s, hr_r, x_s,
):
    r = lax.axis_index("row")
    c = lax.axis_index("col")
    L = C // 2
    line = lax.div(c, 2)
    y = lax.rem(c, 2)
    mate = 2 * line + 1 - y
    c_next, c_prev = lax.rem(c + 1, C), lax.rem(c + C - 1, C)
    r_next, r_prev = lax.rem(r + 1, R), lax.rem(r + R - 1, R)
    can_up, can_down = line < L - 1, line > 0
    c_up, c_down = lax.rem(c + 2, C), lax.rem(c + C - 2, C)
    rows, cols = x.shape
    win = lr_in.shape[2]
    half = win // 2
    nr = rr_in.shape[0]
    nleft = lr_in.shape[0]
    pending = []
    fetch = pltpu.make_async_copy(x_in, x, x_s)
    fetch.start()

    def put(src, dst, ssem, rsem, dev, pred=None):
        def copy():
            return pltpu.make_async_remote_copy(
                src_ref=src(), dst_ref=dst(), send_sem=ssem(), recv_sem=rsem(),
                device_id=dev, device_id_type=MESH,
            )

        run(pred, lambda: copy().start())
        pending.append((pred, lambda: copy().wait_send()))

    def got(dst, rsem, pred=None):
        def wait():
            pltpu.make_async_remote_copy(
                src_ref=dst(), dst_ref=dst(), send_sem=rsem(), recv_sem=rsem(),
                device_id={"col": c_next}, device_id_type=MESH,
            ).wait_recv()

        run(pred, wait)

    barrier = pltpu.get_barrier_semaphore()

    def greet(dev, pred=None):
        run(pred, lambda: pl.semaphore_signal(barrier, inc=1, device_id=dev, device_id_type=MESH))

    for d in range(1, R):
        greet({"row": lax.rem(r + d, R)})
    greet({"col": c_next})
    greet({"col": c_prev})
    greet({"col": c_up}, can_up)
    greet({"col": c_down}, can_down)
    pl.semaphore_wait(barrier, R + 1 + can_up.astype(jnp.int32) + can_down.astype(jnp.int32))

    peers = [lax.rem(r + 2 * d, R) for d in range(1, R // 2)]
    sib = r + 1 - 2 * lax.rem(r, 2)

    def round_rows(src, buf, ss, rs):
        for d, q in enumerate(peers):
            put(src, lambda: buf.at[r], lambda d=d: ss.at[d], lambda: rs.at[r], {"row": q})
        put(src, lambda: buf.at[r], lambda: ss.at[R // 2 - 1], lambda: rs.at[r], {"row": sib})

    def to_sibling(buf, ss, rs):
        for d, q in enumerate(peers):
            got(lambda: buf.at[q], lambda: rs.at[q])
            put(lambda q=q: buf.at[q], lambda q=q: buf.at[q], lambda d=d: ss.at[R // 2 + d],
                lambda q=q: rs.at[q], {"row": sib})

    def from_sibling(buf, rs):
        for q in [sib] + [lax.rem(sib + 2 * d, R) for d in range(1, R // 2)]:
            got(lambda: buf.at[q], lambda: rs.at[q])

    round_rows(lambda: rr_in, rr, rr_s, rr_r)

    def lr_put(src, j, k, dev, pred):
        put(src, lambda: lr.at[j], lambda: lr_s.at[k, j], lambda: lr_r.at[j], {"col": dev}, pred)

    def lo_put(src, j, k, dev, pred):
        put(src, lambda: lo.at[j], lambda: lo_s.at[k, j], lambda: lo_r.at[j], {"col": dev}, pred)

    def nl_put(src, j, pred):
        put(src, lambda: nl.at[j], lambda: nl_s.at[j], lambda: nl_r.at[j], {"row": r_prev}, pred)

    lr_put(lambda: lr_in, c, 2, mate, None)
    lr_put(lambda: lr_in, c, 0, c_up, can_up)
    lr_put(lambda: lr_in, c, 1, c_down, can_down)
    put(lambda: ro_in.at[0, :, pl.ds(0, half)], lambda: nx.at[r], lambda: nx_s.at[R - 1],
        lambda: nx_r.at[r], {"col": c_prev})
    round_rows(lambda: ro_in, ro, ro_s, ro_r)
    lo_put(lambda: lo_in, c, 2, mate, None)
    lo_put(lambda: lo_in, c, 0, c_up, can_up)
    lo_put(lambda: lo_in, c, 1, c_down, can_down)
    nl_put(lambda: lo_in.at[0, :, pl.ds(0, half)], c, None)
    rr[r] = rr_in[...]
    ro[r] = ro_in[...]
    lr[c] = lr_in[...]
    lo[c] = lo_in[...]

    def lr_pass(j, k, dev, pred):
        lr_put(lambda: lr.at[j], j, k, dev, pred)

    def lr_step(s, par):
        below, above = line - 1 - s, line + 1 + s
        jb = lax.rem(2 * below + par + 2 * C, C)
        ja = lax.rem(2 * above + par, C)
        has_b, has_a = below >= 0, above <= L - 1
        got(lambda: lr.at[jb], lambda: lr_r.at[jb], has_b)
        lr_pass(jb, 0, c_up, both(has_b, can_up))
        got(lambda: lr.at[ja], lambda: lr_r.at[ja], has_a)
        lr_pass(ja, 1, c_down, both(has_a, can_down))

    def lo_step(s):
        below, above = line - 1 - s, line + 1 + s
        jb = lax.rem(2 * below + y + 2 * C, C)
        ja = lax.rem(2 * above + y, C)
        has_b, has_a = below >= 0, above <= L - 1
        for j, has, k, dev, can in (
            (jb, has_b, 0, c_up, can_up), (ja, has_a, 1, c_down, can_down),
        ):
            got(lambda: lo.at[j], lambda: lo_r.at[j], has)
            lo_put(lambda j=j: lo.at[j], j, 2, mate, has)
            lo_put(lambda j=j: lo.at[j], j, k, dev, both(has, can))
            nl_put(lambda j=j: lo.at[j, 0, :, pl.ds(0, half)], j, has)

    to_sibling(rr, rr_s, rr_r)
    got(lambda: lr.at[mate], lambda: lr_r.at[mate])
    lr_pass(mate, 0, c_up, can_up)
    lr_pass(mate, 1, c_down, can_down)
    lr_step(0, y)

    from_sibling(rr, rr_r)
    for w in range(nr):
        h, l = split(rr[:, w].reshape(win, win))
        rr_h[w] = h
        rr_l[w] = l
    n_chunks = rows // chunk

    def span(i):
        return pl.ds(pl.multiple_of(i * chunk, chunk), chunk)

    def halo_copies(i):
        right = pltpu.make_async_remote_copy(
            src_ref=m.at[span(i), pl.ds(cols - half, half)], dst_ref=hp.at[span(i), :],
            send_sem=hp_s.at[i], recv_sem=hp_r.at[i],
            device_id={"col": c_next}, device_id_type=MESH)
        left = pltpu.make_async_remote_copy(
            src_ref=m.at[span(i), pl.ds(0, half)], dst_ref=hn.at[span(i), :],
            send_sem=hn_s.at[i], recv_sem=hn_r.at[i],
            device_id={"col": c_prev}, device_id_type=MESH)
        return right, left

    odd = lax.rem(r, 2)

    def turn(i, n):
        return i + odd * (n - 1 - 2 * i)

    def right_chunk(i, carry):
        i = turn(i, n_chunks)
        for w in range(nr):
            a = split(x[span(i), pl.ds(w * win, win)])
            m[span(i), pl.ds(w * win, win)] = dot3(a, (rr_h[w], rr_l[w]), RIGHT)
        for copy in halo_copies(i):
            copy.start()
        return carry

    fetch.wait()
    lax.fori_loop(0, n_chunks, right_chunk, 0)

    got(lambda: nx.at[r], lambda: nx_r.at[r])
    round_rows(lambda: nx.at[r], nx, nx_s, nx_r)

    lr_step(0, 1 - y)
    to_sibling(ro, ro_s, ro_r)
    lo_step(0)
    to_sibling(nx, nx_s, nx_r)
    for s in range(1, L - 1):
        lr_step(s, y)
        lr_step(s, 1 - y)

    from_sibling(ro, ro_r)
    from_sibling(nx, nx_r)
    for w in range(nr):
        h, l = split(ro[:, w].reshape(win, win))
        ro_h[w] = h
        ro_l[w] = l
    h, l = split(nx[...].reshape(win, half))
    nx_h[...] = h
    nx_l[...] = l

    def shifted_chunk(i, carry):
        i = turn(i, n_chunks)
        right, left = halo_copies(i)
        right.wait_recv()
        first = split(m[span(i), pl.ds(0, half)])
        ahead = split(hp[span(i), :])
        top = (ro_h[0, :half, half:], ro_l[0, :half, half:])
        low = (ro_h[0, half:, half:], ro_l[0, half:, half:])
        m2[span(i), pl.ds(0, half)] = dot3(ahead, top, RIGHT) + dot3(first, low, RIGHT)
        for w in range(1, nr):
            a = split(m[span(i), pl.ds(w * win - half, win)])
            m2[span(i), pl.ds(w * win - half, win)] = dot3(a, (ro_h[w], ro_l[w]), RIGHT)
        left.wait_recv()
        last = split(m[span(i), pl.ds(cols - half, half)])
        after = split(hn[span(i), :])
        top = (nx_h[:half, :], nx_l[:half, :])
        low = (nx_h[half:, :], nx_l[half:, :])
        m2[span(i), pl.ds(cols - half, half)] = dot3(last, top, RIGHT) + dot3(after, low, RIGHT)
        return carry

    def left_window(k, carry):
        k = turn(k, nleft)
        at = pl.ds(pl.multiple_of(k * win, win), win)
        q = split(lr[:, k].reshape(win, win))
        for w in range(cols // win):
            across = pl.ds(w * win, win)
            m3[at, across] = dot3(q, split(m2[at, across]), LEFT)
        return carry

    def rows_up(pred):
        put(lambda: m3.at[pl.ds(rows - half, half), :], lambda: ha, lambda: hr_s.at[0],
            lambda: hr_r.at[0], {"row": r_next}, pred)

    def rows_down(pred):
        put(lambda: m3.at[pl.ds(0, half), :], lambda: hb, lambda: hr_s.at[1],
            lambda: hr_r.at[1], {"row": r_prev}, pred)

    per = win // chunk
    lax.fori_loop(0, per, shifted_chunk, 0)
    left_window(0, 0)
    rows_down(odd == 0)
    rows_up(odd == 1)
    def other_windows():
        for k in range(1, nleft):
            lax.fori_loop(k * per, (k + 1) * per, shifted_chunk, 0)
            left_window(k, 0)
        rows_up(odd == 0)
        rows_down(odd == 1)

    for s in range(1, L - 1):
        lo_step(s)
        if s == 1:
            other_windows()
    if L <= 2:
        other_windows()

    for g in range(L):
        j = 2 * g + 1 - y
        got(lambda: lo.at[j], lambda: lo_r.at[j])
        nl_put(lambda j=j: lo.at[j, 0, :, pl.ds(0, half)], j, None)

    def shifted_left(k, carry):
        at = pl.ds(pl.multiple_of(k * win - half, half), win)
        q = split(lo[:, k].reshape(win, win))
        for w in range(cols // win):
            across = pl.ds(w * win, win)
            out[at, across] = dot3(q, split(m3[at, across]), LEFT)
        return carry

    lax.fori_loop(1, nleft, shifted_left, 0)
    got(lambda: ha, lambda: hr_r.at[0])
    q = split(lo[:, 0].reshape(win, win)[:, half:])
    for w in range(cols // win):
        across = pl.ds(w * win, win)
        out[pl.ds(0, half), across] = dot3(
            (q[0][:half], q[1][:half]), split(ha[:, across]), LEFT
        ) + dot3((q[0][half:], q[1][half:]), split(m3[pl.ds(0, half), across]), LEFT)
    for j in range(C):
        got(lambda: nl.at[j], lambda: nl_r.at[j])
    got(lambda: hb, lambda: hr_r.at[1])
    q = split(nl[...].reshape(win, half))
    for w in range(cols // win):
        across = pl.ds(w * win, win)
        out[pl.ds(rows - half, half), across] = dot3(
            (q[0][:half], q[1][:half]), split(m3[pl.ds(rows - half, half), across]), LEFT
        ) + dot3((q[0][half:], q[1][half:]), split(hb[:, across]), LEFT)

    def sent(i, carry):
        for copy in halo_copies(i):
            copy.wait_send()
        return carry

    lax.fori_loop(0, n_chunks, sent, 0)
    for pred, wait in pending:
        run(pred, wait)


def solution(mesh):
    R, C = mesh.shape["row"], mesh.shape["col"]

    def body(schur, left_rot, right_rot, left_off, right_off):
        rows, cols = schur.shape
        win = left_rot.shape[2]
        half = win // 2
        nr, nleft = right_rot.shape[0], left_rot.shape[0]
        chunk = half
        n_chunks = rows // chunk
        dma = pltpu.SemaphoreType.DMA
        vm = pltpu.VMEM
        right = (R,) + right_rot.shape
        left = (C,) + left_rot.shape
        return pl.pallas_call(
            functools.partial(kernel, R, C, chunk),
            out_shape=jax.ShapeDtypeStruct((rows, cols), F32),
            in_specs=[pl.BlockSpec(memory_space=pl.ANY)] + [pl.BlockSpec(memory_space=vm)] * 4,
            out_specs=pl.BlockSpec(memory_space=vm),
            scratch_shapes=[
                vm((rows, cols), F32), vm(right, F32), vm(right, F32), vm((R, win // R, half), F32),
                vm(left, F32), vm(left, F32), vm((C, win // C, half), F32),
                vm((rows, cols), F32), vm((rows, cols), F32), vm((rows, cols), F32),
                vm((rows, half), F32), vm((rows, half), F32),
                vm((half, cols), F32), vm((half, cols), F32),
                vm((nr, win, win), BF16), vm((nr, win, win), BF16),
                vm((nr, win, win), BF16), vm((nr, win, win), BF16),
                vm((win, half), BF16), vm((win, half), BF16),
                dma((R,)), dma((R,)), dma((R,)), dma((R,)), dma((R,)), dma((R,)),
                dma((3, C)), dma((C,)), dma((3, C)), dma((C,)), dma((C,)), dma((C,)),
                dma((n_chunks,)), dma((n_chunks,)), dma((n_chunks,)), dma((n_chunks,)),
                dma((2,)), dma((2,)), dma,
            ],
            compiler_params=pltpu.CompilerParams(collective_id=0, has_side_effects=True),
        )(schur, right_rot, right_off, left_rot, left_off)

    return jax.shard_map(
        body,
        mesh=mesh,
        in_specs=(
            P("row", "col"),
            P("row", "col", None),
            P("col", "row", None),
            P("row", "col", None),
            P("col", "row", None),
        ),
        out_specs=P("row", "col"),
        check_vma=False,
    )
```

```python
import functools

import jax
import jax.numpy as jnp
from jax import lax
from jax.experimental import pallas as pl
from jax.experimental.pallas import tpu as pltpu
from jax.sharding import PartitionSpec as P

MESH = pl.DeviceIdType.MESH
F32 = jnp.float32
BF16 = jnp.bfloat16


def run(pred, fn):
    if pred is None:
        fn()
    else:
        pl.when(pred)(fn)


def both(a, b):
    if a is None:
        return b
    if b is None:
        return a
    return jnp.logical_and(a, b)


def split(v):
    high = v.astype(BF16)
    return high, (v - high.astype(F32)).astype(BF16)


def dot3(a, b, dims):
    def one(p, q):
        return lax.dot_general(p, q, (dims, ((), ())), preferred_element_type=F32)

    return one(a[0], b[0]) + (one(a[0], b[1]) + one(a[1], b[0]))


RIGHT = ((1,), (0,))
LEFT = ((0,), (0,))


def kernel(
    R, C, chunk,
    x_in, rr_in, ro_in, lr_in, lo_in, out,
    x, rr, ro, nx, lr, lo, nl, m, m2, m3, hp, hn, ha, hb,
    rr_h, rr_l, ro_h, ro_l, nx_h, nx_l,
    rr_s, rr_r, ro_s, ro_r, nx_s, nx_r, lr_s, lr_r, lo_s, lo_r, nl_s, nl_r,
    hp_s, hp_r, hn_s, hn_r, hr_s, hr_r, x_s,
):
    r = lax.axis_index("row")
    c = lax.axis_index("col")
    L = C // 2
    line = lax.div(c, 2)
    y = lax.rem(c, 2)
    mate = 2 * line + 1 - y
    c_next, c_prev = lax.rem(c + 1, C), lax.rem(c + C - 1, C)
    r_next, r_prev = lax.rem(r + 1, R), lax.rem(r + R - 1, R)
    can_up, can_down = line < L - 1, line > 0
    c_up, c_down = lax.rem(c + 2, C), lax.rem(c + C - 2, C)
    rows, cols = x.shape
    win = lr_in.shape[2]
    half = win // 2
    nr = rr_in.shape[0]
    nleft = lr_in.shape[0]
    pending = []
    fetch = pltpu.make_async_copy(x_in, x, x_s)
    fetch.start()

    def put(src, dst, ssem, rsem, dev, pred=None):
        def copy():
            return pltpu.make_async_remote_copy(
                src_ref=src(), dst_ref=dst(), send_sem=ssem(), recv_sem=rsem(),
                device_id=dev, device_id_type=MESH,
            )

        run(pred, lambda: copy().start())
        pending.append((pred, lambda: copy().wait_send()))

    def got(dst, rsem, pred=None):
        def wait():
            pltpu.make_async_remote_copy(
                src_ref=dst(), dst_ref=dst(), send_sem=rsem(), recv_sem=rsem(),
                device_id={"col": c_next}, device_id_type=MESH,
            ).wait_recv()

        run(pred, wait)

    barrier = pltpu.get_barrier_semaphore()

    def greet(dev, pred=None):
        run(pred, lambda: pl.semaphore_signal(barrier, inc=1, device_id=dev, device_id_type=MESH))

    for d in range(1, R):
        greet({"row": lax.rem(r + d, R)})
    greet({"col": c_next})
    greet({"col": c_prev})
    greet({"col": c_up}, can_up)
    greet({"col": c_down}, can_down)
    pl.semaphore_wait(barrier, R + 1 + can_up.astype(jnp.int32) + can_down.astype(jnp.int32))

    peers = [lax.rem(r + 2 * d, R) for d in range(1, R // 2)]
    sib = r + 1 - 2 * lax.rem(r, 2)

    def round_rows(src, buf, ss, rs):
        for d, q in enumerate(peers):
            put(src, lambda: buf.at[r], lambda d=d: ss.at[d], lambda: rs.at[r], {"row": q})
        put(src, lambda: buf.at[r], lambda: ss.at[R // 2 - 1], lambda: rs.at[r], {"row": sib})

    def to_sibling(buf, ss, rs):
        for d, q in enumerate(peers):
            got(lambda: buf.at[q], lambda: rs.at[q])
            put(lambda q=q: buf.at[q], lambda q=q: buf.at[q], lambda d=d: ss.at[R // 2 + d],
                lambda q=q: rs.at[q], {"row": sib})

    def from_sibling(buf, rs):
        for q in [sib] + [lax.rem(sib + 2 * d, R) for d in range(1, R // 2)]:
            got(lambda: buf.at[q], lambda: rs.at[q])

    round_rows(lambda: rr_in, rr, rr_s, rr_r)

    def lr_put(src, j, k, dev, pred):
        put(src, lambda: lr.at[j], lambda: lr_s.at[k, j], lambda: lr_r.at[j], {"col": dev}, pred)

    def lo_put(src, j, k, dev, pred):
        put(src, lambda: lo.at[j], lambda: lo_s.at[k, j], lambda: lo_r.at[j], {"col": dev}, pred)

    def nl_put(src, j, pred):
        put(src, lambda: nl.at[j], lambda: nl_s.at[j], lambda: nl_r.at[j], {"row": r_prev}, pred)

    lr_put(lambda: lr_in, c, 2, mate, None)
    lr_put(lambda: lr_in, c, 0, c_up, can_up)
    lr_put(lambda: lr_in, c, 1, c_down, can_down)
    put(lambda: ro_in.at[0, :, pl.ds(0, half)], lambda: nx.at[r], lambda: nx_s.at[R - 1],
        lambda: nx_r.at[r], {"col": c_prev})
    round_rows(lambda: ro_in, ro, ro_s, ro_r)
    lo_put(lambda: lo_in, c, 2, mate, None)
    nl_put(lambda: lo_in.at[0, :, pl.ds(0, half)], c, None)
    rr[r] = rr_in[...]
    ro[r] = ro_in[...]
    lr[c] = lr_in[...]
    lo[c] = lo_in[...]

    def lr_pass(j, k, dev, pred):
        lr_put(lambda: lr.at[j], j, k, dev, pred)

    def lr_step(s, par):
        below, above = line - 1 - s, line + 1 + s
        jb = lax.rem(2 * below + par + 2 * C, C)
        ja = lax.rem(2 * above + par, C)
        has_b, has_a = below >= 0, above <= L - 1
        got(lambda: lr.at[jb], lambda: lr_r.at[jb], has_b)
        lr_pass(jb, 0, c_up, both(has_b, can_up))
        got(lambda: lr.at[ja], lambda: lr_r.at[ja], has_a)
        lr_pass(ja, 1, c_down, both(has_a, can_down))

    def lo_step(s):
        below, above = line - 1 - s, line + 1 + s
        jb = lax.rem(2 * below + y + 2 * C, C)
        ja = lax.rem(2 * above + y, C)
        has_b, has_a = below >= 0, above <= L - 1
        for j, has, k, dev, can in (
            (jb, has_b, 0, c_up, can_up), (ja, has_a, 1, c_down, can_down),
        ):
            got(lambda: lo.at[j], lambda: lo_r.at[j], has)
            lo_put(lambda j=j: lo.at[j], j, 2, mate, has)
            lo_put(lambda j=j: lo.at[j], j, k, dev, both(has, can))
            nl_put(lambda j=j: lo.at[j, 0, :, pl.ds(0, half)], j, has)

    to_sibling(rr, rr_s, rr_r)
    got(lambda: lr.at[mate], lambda: lr_r.at[mate])
    lr_pass(mate, 0, c_up, can_up)
    lr_pass(mate, 1, c_down, can_down)
    lr_step(0, y)

    from_sibling(rr, rr_r)
    for w in range(nr):
        h, l = split(rr[:, w].reshape(win, win))
        rr_h[w] = h
        rr_l[w] = l
    n_chunks = rows // chunk

    def span(i):
        return pl.ds(pl.multiple_of(i * chunk, chunk), chunk)

    def halo_copies(i):
        right = pltpu.make_async_remote_copy(
            src_ref=m.at[span(i), pl.ds(cols - half, half)], dst_ref=hp.at[span(i), :],
            send_sem=hp_s.at[i], recv_sem=hp_r.at[i],
            device_id={"col": c_next}, device_id_type=MESH)
        left = pltpu.make_async_remote_copy(
            src_ref=m.at[span(i), pl.ds(0, half)], dst_ref=hn.at[span(i), :],
            send_sem=hn_s.at[i], recv_sem=hn_r.at[i],
            device_id={"col": c_prev}, device_id_type=MESH)
        return right, left

    odd = lax.rem(r, 2)

    def turn(i, n):
        return i + odd * (n - 1 - 2 * i)

    def right_chunk(i, carry):
        i = turn(i, n_chunks)
        for w in range(nr):
            a = split(x[span(i), pl.ds(w * win, win)])
            m[span(i), pl.ds(w * win, win)] = dot3(a, (rr_h[w], rr_l[w]), RIGHT)
        for copy in halo_copies(i):
            copy.start()
        return carry

    fetch.wait()
    lax.fori_loop(0, n_chunks, right_chunk, 0)

    got(lambda: nx.at[r], lambda: nx_r.at[r])
    round_rows(lambda: nx.at[r], nx, nx_s, nx_r)

    lr_step(0, 1 - y)
    lo_put(lambda: lo_in, c, 0, c_up, can_up)
    lo_put(lambda: lo_in, c, 1, c_down, can_down)
    to_sibling(ro, ro_s, ro_r)
    lo_step(0)
    to_sibling(nx, nx_s, nx_r)
    for s in range(1, L - 2):
        lr_step(s, y)
        lr_step(s, 1 - y)

    from_sibling(ro, ro_r)
    from_sibling(nx, nx_r)
    for w in range(nr):
        h, l = split(ro[:, w].reshape(win, win))
        ro_h[w] = h
        ro_l[w] = l
    h, l = split(nx[...].reshape(win, half))
    nx_h[...] = h
    nx_l[...] = l

    def shifted_chunk(i, carry):
        i = turn(i, n_chunks)
        right, left = halo_copies(i)
        right.wait_recv()
        first = split(m[span(i), pl.ds(0, half)])
        ahead = split(hp[span(i), :])
        top = (ro_h[0, :half, half:], ro_l[0, :half, half:])
        low = (ro_h[0, half:, half:], ro_l[0, half:, half:])
        m2[span(i), pl.ds(0, half)] = dot3(ahead, top, RIGHT) + dot3(first, low, RIGHT)
        for w in range(1, nr):
            a = split(m[span(i), pl.ds(w * win - half, win)])
            m2[span(i), pl.ds(w * win - half, win)] = dot3(a, (ro_h[w], ro_l[w]), RIGHT)
        left.wait_recv()
        last = split(m[span(i), pl.ds(cols - half, half)])
        after = split(hn[span(i), :])
        top = (nx_h[:half, :], nx_l[:half, :])
        low = (nx_h[half:, :], nx_l[half:, :])
        m2[span(i), pl.ds(cols - half, half)] = dot3(last, top, RIGHT) + dot3(after, low, RIGHT)
        return carry

    per = win // chunk
    lax.fori_loop(0, per, shifted_chunk, 0)
    if L > 2:
        lr_step(L - 2, y)
        lo_step(1)
        lr_step(L - 2, 1 - y)

    def left_window(k, carry):
        k = turn(k, nleft)
        at = pl.ds(pl.multiple_of(k * win, win), win)
        q = split(lr[:, k].reshape(win, win))
        for w in range(cols // win):
            across = pl.ds(w * win, win)
            m3[at, across] = dot3(q, split(m2[at, across]), LEFT)
        return carry

    def rows_up(pred):
        put(lambda: m3.at[pl.ds(rows - half, half), :], lambda: ha, lambda: hr_s.at[0],
            lambda: hr_r.at[0], {"row": r_next}, pred)

    def rows_down(pred):
        put(lambda: m3.at[pl.ds(0, half), :], lambda: hb, lambda: hr_s.at[1],
            lambda: hr_r.at[1], {"row": r_prev}, pred)

    left_window(0, 0)
    rows_down(odd == 0)
    rows_up(odd == 1)
    def other_windows():
        for k in range(1, nleft):
            lax.fori_loop(k * per, (k + 1) * per, shifted_chunk, 0)
            left_window(k, 0)
        rows_up(odd == 0)
        rows_down(odd == 1)

    other_windows()
    for s in range(2, L - 1):
        lo_step(s)

    strip = win // C

    def stack(ref, at, par):
        return jnp.concatenate(
            [ref[pl.ds(pl.multiple_of(at + (2 * g + par) * strip, strip), strip), :]
             for g in range(L // 2)], axis=0)

    def product(q, parts, at, add):
        b = split(jnp.concatenate(parts, axis=0))
        res = dot3(split(q), b, LEFT)
        out[at, :] = out[at, :] + res if add else res

    def off(k, par, lo_cut, hi_cut):
        return jnp.concatenate([lo[2 * g + par, k, :, lo_cut:hi_cut] for g in range(L)], axis=0)

    def middle(par, add):
        for k in range(1, nleft):
            base = k * win - half
            product(off(k, par, 0, win),
                    [stack(m3, base, par), stack(m3, k * win, par)], pl.ds(base, win), add)

    def leading(par, add):
        product(off(0, par, half, win),
                [stack(ha, 0, par), stack(m3, 0, par)], pl.ds(0, half), add)

    def trailing(par, add):
        q = jnp.concatenate([nl[2 * g + par] for g in range(L)], axis=0)
        product(q, [stack(m3, rows - half, par), stack(hb, 0, par)],
                pl.ds(rows - half, half), add)

    middle(y, False)
    got(lambda: ha, lambda: hr_r.at[0])
    leading(y, False)
    for g in range(L):
        j = 2 * g + y
        got(lambda: nl.at[j], lambda: nl_r.at[j])
    got(lambda: hb, lambda: hr_r.at[1])
    trailing(y, False)
    for g in range(L):
        j = 2 * g + 1 - y
        got(lambda: lo.at[j], lambda: lo_r.at[j])
        nl_put(lambda j=j: lo.at[j, 0, :, pl.ds(0, half)], j, None)
    middle(1 - y, True)
    leading(1 - y, True)
    for g in range(L):
        j = 2 * g + 1 - y
        got(lambda: nl.at[j], lambda: nl_r.at[j])
    trailing(1 - y, True)

    def sent(i, carry):
        for copy in halo_copies(i):
            copy.wait_send()
        return carry

    lax.fori_loop(0, n_chunks, sent, 0)
    for pred, wait in pending:
        run(pred, wait)


def solution(mesh):
    R, C = mesh.shape["row"], mesh.shape["col"]

    def body(schur, left_rot, right_rot, left_off, right_off):
        rows, cols = schur.shape
        win = left_rot.shape[2]
        half = win // 2
        nr, nleft = right_rot.shape[0], left_rot.shape[0]
        chunk = half
        n_chunks = rows // chunk
        dma = pltpu.SemaphoreType.DMA
        vm = pltpu.VMEM
        right = (R,) + right_rot.shape
        left = (C,) + left_rot.shape
        return pl.pallas_call(
            functools.partial(kernel, R, C, chunk),
            out_shape=jax.ShapeDtypeStruct((rows, cols), F32),
            in_specs=[pl.BlockSpec(memory_space=pl.ANY)] + [pl.BlockSpec(memory_space=vm)] * 4,
            out_specs=pl.BlockSpec(memory_space=vm),
            scratch_shapes=[
                vm((rows, cols), F32), vm(right, F32), vm(right, F32), vm((R, win // R, half), F32),
                vm(left, F32), vm(left, F32), vm((C, win // C, half), F32),
                vm((rows, cols), F32), vm((rows, cols), F32), vm((rows, cols), F32),
                vm((rows, half), F32), vm((rows, half), F32),
                vm((half, cols), F32), vm((half, cols), F32),
                vm((nr, win, win), BF16), vm((nr, win, win), BF16),
                vm((nr, win, win), BF16), vm((nr, win, win), BF16),
                vm((win, half), BF16), vm((win, half), BF16),
                dma((R,)), dma((R,)), dma((R,)), dma((R,)), dma((R,)), dma((R,)),
                dma((3, C)), dma((C,)), dma((3, C)), dma((C,)), dma((C,)), dma((C,)),
                dma((n_chunks,)), dma((n_chunks,)), dma((n_chunks,)), dma((n_chunks,)),
                dma((2,)), dma((2,)), dma,
            ],
            compiler_params=pltpu.CompilerParams(collective_id=0, has_side_effects=True),
        )(schur, right_rot, right_off, left_rot, left_off)

    return jax.shard_map(
        body,
        mesh=mesh,
        in_specs=(
            P("row", "col"),
            P("row", "col", None),
            P("col", "row", None),
            P("row", "col", None),
            P("col", "row", None),
        ),
        out_specs=P("row", "col"),
        check_vma=False,
    )
```
